32 devices in a mesh: groups: 2 (over x), wide: 16 (over z, y, core).
Axes of the slice: x: 2, y: 2, z: 4, core: 2. Of those that a mesh axis runs over, the one named last changes fastest.
Arguments:
- fine_field: float32 [256, 64, 512], P(None, ('groups', 'wide')), parts along dimension 1, may hold values from -6 to 6
- w_down_fine: float32 [8, 256, 512], replicated, may hold values from -0.125 to 0.125
- w_conv_mid: float32 [27, 512, 512], P(None, 'wide'), may hold values from -0.0546875 to 0.0546875
- w_down_mid: float32 [8, 512, 1024], P(None, 'wide'), may hold values from -0.09375 to 0.09375
- w_conv_deep: float32 [27, 1024, 1024], P(None, 'wide'), may hold values from -0.0390625 to 0.0390625
- w_up_deep: float32 [8, 1024, 512], P(None, 'wide'), may hold values from -0.1875 to 0.1875
- w_up_mid: float32 [8, 512, 256], replicated, may hold values from -0.25 to 0.25
Outputs:
- fine_update: float32 [256, 64, 512], P(None, ('groups', 'wide')), parts along dimension 1
The draws below stay inside these ranges and needn't reach their ends.
There are 2 independent parts, one for each index of `groups`. The reference program is written for one: setup_inputs(seed, part) draws one part's arguments, and reference() takes and returns one part's arrays. A program takes and returns all parts, laid end to end along the dimension named above; an argument that names none is the same for every part. Nothing has to cross between parts.
All inputs are finite; a program needn't handle non-finite values.
Results may differ from the reference program's by a relative error of at most 0.0001.
Values sent between devices are 32-bit elements; how exact they have to be, the bound alone decides.
No kernel may reach another device: no remote copies, remote signals or barrier semaphores. Data moves between devices by JAX's collectives and lax.ppermute only.
A program may use at most 192 MiB of HBM per device.

```python
import jax
import jax.numpy as jnp
from jax import lax

CA = 256
CB = 512
CC = 1024
YA = 32
ZA = 16
NXA = 32


def steps_of(stream_key, dims, split, least, top_value):
    level = 1.0
    for axis_at, parts in split:
        steps = jax.random.uniform(jax.random.fold_in(jax.random.fold_in(stream_key, 6), axis_at), (parts,), jnp.float32, least / len(split), top_value / len(split))
        level = level * jnp.repeat(jnp.exp(steps), dims[axis_at] // parts).reshape((-1,) + (1,) * (len(dims) - 1 - axis_at))
    return level


def bell_draw(own_key, dims, deviation, bound, split=(), dtype=jnp.bfloat16):
    drawn = deviation * jax.random.normal(own_key, dims, jnp.float32)
    if split:
        drawn = drawn * steps_of(own_key, dims, split, -0.22, 0.18)
    return jnp.clip(drawn, -bound, bound).astype(dtype)


def setup_inputs(seed: int = 0, part: int = 0) -> dict:
    arg_keys = jax.random.split(jax.random.key(seed), 8)
    part_keys = jax.random.split(jax.random.fold_in(arg_keys[7], part), 8)
    fine_field = bell_draw(part_keys[0], (CA, NXA, YA * ZA), 1.0, 6.0, ((1, 16),), jnp.float32)
    w_down_fine = bell_draw(arg_keys[1], (8, CA, CB), (8 * CA) ** -0.5, 0.125, (), jnp.float32)
    w_conv_mid = bell_draw(arg_keys[2], (27, CB, CB), (27 * CB) ** -0.5, 0.0546875, ((1, 16),), jnp.float32)
    w_down_mid = bell_draw(arg_keys[3], (8, CB, CC), (8 * CB) ** -0.5, 0.09375, ((1, 16),), jnp.float32)
    w_conv_deep = bell_draw(arg_keys[4], (27, CC, CC), (27 * CC) ** -0.5, 0.0390625, ((1, 16),), jnp.float32)
    w_up_deep = bell_draw(arg_keys[5], (8, CC, CB), CC ** -0.5, 0.1875, ((1, 16),), jnp.float32)
    w_up_mid = bell_draw(arg_keys[6], (8, CB, CA), CB ** -0.5, 0.25, (), jnp.float32)
    return dict(fine_field=fine_field, w_down_fine=w_down_fine, w_conv_mid=w_conv_mid, w_down_mid=w_down_mid, w_conv_deep=w_conv_deep, w_up_deep=w_up_deep, w_up_mid=w_up_mid)


HIGHEST_MODE = lax.Precision.HIGHEST


def convolve_three(field, weights):
    planes, rows, cols = field.shape[1], field.shape[2], field.shape[3]
    padded = jnp.pad(field, ((0, 0), (1, 1), (1, 1), (1, 1)))
    summed = jnp.zeros((weights.shape[1], planes, rows, cols), jnp.float32)
    for a in range(3):
        for b in range(3):
            for c in range(3):
                window = padded[:, a:a + planes, b:b + rows, c:c + cols]
                summed = summed + jnp.einsum("oc,cxyz->oxyz", weights[9 * a + 3 * b + c], window, precision=HIGHEST_MODE)
    return summed


def stride_down(field, weights):
    summed = jnp.zeros((weights.shape[2], field.shape[1] // 2, field.shape[2] // 2, field.shape[3] // 2), jnp.float32)
    for a in range(2):
        for b in range(2):
            for c in range(2):
                window = field[:, a::2, b::2, c::2]
                summed = summed + jnp.einsum("co,cxyz->oxyz", weights[4 * a + 2 * b + c], window, precision=HIGHEST_MODE)
    return summed


def stride_up(field, weights):
    outputs = weights.shape[2]
    planes, rows, cols = field.shape[1], field.shape[2], field.shape[3]
    pieces = [jnp.einsum("co,cxyz->oxyz", weights[tap], field, precision=HIGHEST_MODE) for tap in range(8)]
    stacked = jnp.stack(pieces).reshape(2, 2, 2, outputs, planes, rows, cols)
    return stacked.transpose(3, 4, 0, 5, 1, 6, 2).reshape(outputs, 2 * planes, 2 * rows, 2 * cols)


def reference(fine_field, w_down_fine, w_conv_mid, w_down_mid, w_conv_deep, w_up_deep, w_up_mid):
    fine = fine_field.reshape(CA, NXA, YA, ZA)
    mid_input = stride_down(fine, w_down_fine)
    mid_field = jax.nn.relu(convolve_three(mid_input, w_conv_mid))
    deep_input = jax.nn.relu(stride_down(mid_field, w_down_mid))
    deep_output = jax.nn.relu(convolve_three(deep_input, w_conv_deep))
    mid_merged = jax.nn.relu(mid_field + stride_up(deep_output, w_up_deep))
    fine_update = stride_up(mid_merged, w_up_mid)
    return fine_update.reshape(CA, NXA, YA * ZA)
```

```python
import functools

import jax
import jax.numpy as jnp
from jax import lax
from jax.experimental import pallas as pl
from jax.experimental.pallas import tpu as pltpu
from jax.sharding import PartitionSpec as P

YA = 32
ZA = 16
MID_ROWS, MID_COLS = YA // 2, ZA // 2
MID_CELLS = MID_ROWS * MID_COLS
DEEP_ROWS, DEEP_COLS = YA // 4, ZA // 4
DEEP_CELLS = DEEP_ROWS * DEEP_COLS
LANES = 128
PACK = LANES // DEEP_CELLS
SMEM = pl.BlockSpec(memory_space=pltpu.SMEM)
VMEM = pl.BlockSpec(memory_space=pltpu.VMEM)


def split_outside(weights):
    rounded = lax.reduce_precision(weights, 8, 7)
    return rounded.astype(jnp.bfloat16), (weights - rounded).astype(jnp.bfloat16)


def split_inside(values):
    high = values.astype(jnp.bfloat16)
    return high, (values - high.astype(jnp.float32)).astype(jnp.bfloat16)


def product(left, right):
    return jnp.dot(left, right, preferred_element_type=jnp.float32)


def product_three(left_high, left_low, right_high, right_low):
    return (
        product(left_high, right_high)
        + product(left_high, right_low)
        + product(left_low, right_high)
    )


def picker(blocks, rows, cols):
    small_rows, small_cols = rows // 2, cols // 2
    big = jnp.arange(blocks * rows * cols)[:, None]
    small = jnp.arange(4 * blocks * small_rows * small_cols)[None, :]
    cells = small_rows * small_cols
    tap, block, cell = small // (blocks * cells), small // cells % blocks, small % cells
    row = 2 * (cell // small_cols) + tap // 2
    col = 2 * (cell % small_cols) + tap % 2
    return (big == (block * rows + row) * cols + col).astype(jnp.bfloat16)


def inside(places, limit, step):
    moved = places + step
    return (moved >= 0) & (moved < limit)


def down_fine_kernel(field_ref, place_ref, weight_ref, out_ref, total_ref):
    step = pl.program_id(0)

    def gather(a):
        high, low = split_inside(field_ref[:, a, :])
        return [
            lax.dot_general(place_ref[...], part, (((1,), (1,)), ((), ())), preferred_element_type=jnp.float32).astype(
                jnp.bfloat16
            )
            for part in (high, low)
        ]

    for a in range(2):

        @pl.when(step == a)
        def _():
            high, low = gather(a)
            total = jnp.zeros(total_ref.shape, jnp.float32) if a == 0 else total_ref[...]
            for tap in range(4):
                weight_high, weight_low = split_inside(weight_ref[tap])
                block = slice(tap * MID_CELLS, (tap + 1) * MID_CELLS)
                total = total + product_three(high[block], low[block], weight_high, weight_low)
            if a == 0:
                total_ref[...] = total
            else:
                out_ref[...] = total.T


def down_fine(field, place, weights):
    chan_fine, chan_mid = weights.shape[1:]
    return pl.pallas_call(
        down_fine_kernel,
        out_shape=jax.ShapeDtypeStruct((chan_mid, MID_CELLS), jnp.float32),
        grid=(2,),
        in_specs=[
            pl.BlockSpec(field.shape, lambda a: (0, 0, 0)),
            pl.BlockSpec(place.shape, lambda a: (0, 0)),
            pl.BlockSpec((4, chan_fine, chan_mid), lambda a: (a, 0, 0)),
        ],
        out_specs=pl.BlockSpec((chan_mid, MID_CELLS), lambda a: (0, 0)),
        scratch_shapes=[pltpu.VMEM((MID_CELLS, chan_mid), jnp.float32)],
        name="down_fine",
    )(field, place, weights)


def plane_at(me, step, other, chips):
    chip, core = me // 2, me % 2
    position = jnp.where(chip % 2 == 0, chip // 2, chips - 1 - chip // 2)
    position = (position + step + chips) % chips
    chip = jnp.where(position < chips // 2, 2 * position, 2 * (chips - 1 - position) + 1)
    return 2 * chip + (1 - core if other else core)


def conv_mid_add(me, chips, places, high_ref, low_ref, fields, sum_ref):
    rows = sum_ref.shape[1]
    field_high, field_low = split_inside(jnp.concatenate(fields, axis=1))
    place = lax.broadcasted_iota(jnp.int32, (rows, LANES), 1)
    row_of, col_of = place // MID_COLS, place % MID_COLS
    for a in range(3):
        block = pl.ds(a * 9 * rows, 9 * rows)
        spread = product_three(high_ref[block, :], low_ref[block, :], field_high, field_low)
        for side, (step, other) in enumerate(places):
            total = jnp.zeros((rows, LANES), jnp.float32)
            for b in range(3):
                for c in range(3):
                    tap = 3 * b + c
                    piece = spread[tap * rows : (tap + 1) * rows, side * LANES : (side + 1) * LANES]
                    offset = (b - 1) * MID_COLS + (c - 1)
                    if offset:
                        piece = pltpu.roll(piece, (-offset) % LANES, 1)
                        keep = inside(row_of, MID_ROWS, b - 1) & inside(col_of, MID_COLS, c - 1)
                        piece = jnp.where(keep, piece, 0.0)
                    total = total + piece
            plane = plane_at(me, step, other, chips) + (2 - a)
            sum_ref[plane] = sum_ref[plane] + total


def join(pieces):
    return pieces[0][...] if len(pieces) == 1 else jnp.concatenate([piece[...] for piece in pieces], axis=0)


def conv_mid_kernel(chips, places, parts, first, me_ref, high_ref, low_ref, *refs):
    sum_ref = refs[-1]
    if first:
        sum_ref[...] = jnp.zeros_like(sum_ref)
    else:
        sum_ref[...] = refs[-2][...]
    fields, at = [], 0
    for count in parts:
        fields.append(join(refs[at : at + count]))
        at += count
    conv_mid_add(me_ref[0], chips, places, high_ref, low_ref, fields, sum_ref)


def conv_mid(me, high, low, given, running, planes):
    rows = high.shape[0] // 27
    places = [(step, other) for _, step, other in given]
    fields = [piece for pieces, _, _ in given for piece in pieces]
    parts = [len(pieces) for pieces, _, _ in given]
    arrays = [me, high, low] + fields + ([] if running is None else [running])
    return pl.pallas_call(
        functools.partial(conv_mid_kernel, planes // 2, places, parts, running is None),
        out_shape=jax.ShapeDtypeStruct((planes + 2, rows, LANES), jnp.float32),
        in_specs=[SMEM] + [VMEM] * (len(arrays) - 1),
        out_specs=VMEM,
        input_output_aliases={} if running is None else {len(arrays) - 1: 0},
        name="conv_mid",
    )(*arrays)


def down_mid_kernel(chips, places, parts, me_ref, high_ref, low_ref, pick_ref, weight_ref, *refs):
    running_ref, mid_ref, part_ref, sum_ref = refs[-4:]
    sum_ref[...] = running_ref[...]
    fields, at = [], 0
    for count in parts:
        fields.append(join(refs[at : at + count]))
        at += count
    conv_mid_add(me_ref[0], chips, places, high_ref, low_ref, fields, sum_ref)
    planes = mid_ref.shape[0]
    groups = planes // 2 // PACK
    mid_ref[...] = jnp.maximum(sum_ref[1 : planes + 1], 0.0)
    rows = mid_ref.shape[1]
    lines = []
    for a in range(2):
        for g in range(groups):
            lines.append(jnp.concatenate([mid_ref[2 * (g * PACK + q) + a] for q in range(PACK)], axis=1))
    high, low = split_inside(jnp.concatenate(lines, axis=0))
    picks = []
    for part in (high, low):
        moved = product(part, pick_ref[...]).astype(jnp.bfloat16)
        taps = []
        for a in range(2):
            for tap in range(4):
                taps.append(
                    jnp.concatenate(
                        [
                            moved[(a * groups + g) * rows : (a * groups + g + 1) * rows, tap * LANES : (tap + 1) * LANES]
                            for g in range(groups)
                        ],
                        axis=1,
                    )
                )
        picks.append(jnp.concatenate(taps, axis=0))
    weight_high, weight_low = split_inside(weight_ref[...])
    part_ref[...] = product_three(weight_high, weight_low, picks[0], picks[1])


def down_mid(me, high, low, pick, weight, given, running, planes):
    rows = high.shape[0] // 27
    places = [(step, other) for _, step, other in given]
    fields = [piece for pieces, _, _ in given for piece in pieces]
    parts = [len(pieces) for pieces, _, _ in given]
    arrays = [me, high, low, pick, weight] + fields + [running]
    return pl.pallas_call(
        functools.partial(down_mid_kernel, planes // 2, places, parts),
        out_shape=(
            jax.ShapeDtypeStruct((planes, rows, LANES), jnp.float32),
            jax.ShapeDtypeStruct((weight.shape[0], planes // 2 * DEEP_CELLS), jnp.float32),
        ),
        in_specs=[SMEM] + [VMEM] * (len(arrays) - 1),
        out_specs=(VMEM, VMEM),
        scratch_shapes=[pltpu.VMEM(running.shape, jnp.float32)],
        name="down_mid",
    )(*arrays)


def reversed_bits(value, blocks):
    width = blocks.bit_length() - 1
    return sum(((value >> k) & 1) << (width - 1 - k) for k in range(width))


def sorted_split(me, field_ref, high_ref, low_ref, blocks, whole):
    size = field_ref.shape[0] // blocks
    for block in range(blocks):
        source = reversed_bits(block ^ me, blocks) if whole else block ^ reversed_bits(me % blocks, blocks)
        source = pl.multiple_of(source * size, size)
        high, low = split_inside(field_ref[pl.ds(source, size), :])
        high_ref[pl.ds(block * size, size), :] = high
        low_ref[pl.ds(block * size, size), :] = low


def conv_deep_kernel(blocks, me_ref, weight_ref, field_ref, out_ref, field_high, field_low):
    a = pl.program_id(0)
    rows, cells = out_ref.shape

    @pl.when(a == 0)
    def _():
        sorted_split(me_ref[0], field_ref, field_high, field_low, blocks, False)
        out_ref[...] = jnp.zeros_like(out_ref)

    weight_high, weight_low = split_inside(weight_ref[...])
    spread = product_three(weight_high, weight_low, field_high[...], field_low[...])
    place = lax.broadcasted_iota(jnp.int32, (rows, cells), 1)
    plane_of = place // DEEP_CELLS
    row_of, col_of = place // DEEP_COLS % DEEP_ROWS, place % DEEP_COLS
    total = jnp.zeros((rows, cells), jnp.float32)
    for b in range(3):
        for c in range(3):
            tap = 3 * b + c
            piece = spread[tap * rows : (tap + 1) * rows]
            offset = (b - 1) * DEEP_COLS + (c - 1)
            if offset:
                piece = pltpu.roll(piece, (-offset) % cells, 1)
                keep = inside(row_of, DEEP_ROWS, b - 1) & inside(col_of, DEEP_COLS, c - 1)
                piece = jnp.where(keep, piece, 0.0)
            total = total + piece
    for step in range(3):

        @pl.when(a == step)
        def _():
            moved = total
            if step != 1:
                moved = pltpu.roll(moved, (-(step - 1) * DEEP_CELLS) % cells, 1)
                moved = jnp.where(inside(plane_of, cells // DEEP_CELLS, step - 1), moved, 0.0)
            summed = out_ref[...] + moved
            out_ref[...] = jnp.maximum(summed, 0.0) if step == 2 else summed


def conv_deep(me, blocks, weight, field):
    rows = weight.shape[0] // 27
    depth, cells = field.shape
    return pl.pallas_call(
        functools.partial(conv_deep_kernel, blocks),
        out_shape=jax.ShapeDtypeStruct((rows, cells), jnp.float32),
        grid=(3,),
        in_specs=[
            SMEM,
            pl.BlockSpec((9 * rows, depth), lambda a: (a, 0)),
            pl.BlockSpec((depth, cells), lambda a: (0, 0)),
        ],
        out_specs=pl.BlockSpec((rows, cells), lambda a: (0, 0)),
        scratch_shapes=[pltpu.VMEM((depth, cells), jnp.bfloat16)] * 2,
        name="conv_deep",
    )(me, weight, field)


def up_deep_kernel(blocks, me_ref, weight_ref, field_ref, place_ref, mid_ref, out_ref, field_high, field_low):
    sorted_split(me_ref[0], field_ref, field_high, field_low, blocks, True)
    planes, rows, _ = mid_ref.shape
    groups = planes // 2 // PACK
    size = weight_ref.shape[2] // 8
    weight = jnp.concatenate(
        [
            jnp.concatenate([weight_ref[block, :, tap * size : (tap + 1) * size] for block in range(blocks)], axis=1)
            for tap in range(8)
        ],
        axis=0,
    )
    weight_high, weight_low = split_inside(weight)
    spread = product_three(weight_high, weight_low, field_high[...], field_low[...])
    lines = []
    for a in range(2):
        for g in range(groups):
            lines.append(
                jnp.concatenate(
                    [
                        spread[(4 * a + tap) * rows : (4 * a + tap + 1) * rows, g * LANES : (g + 1) * LANES]
                        for tap in range(4)
                    ],
                    axis=1,
                )
            )
    high, low = split_inside(jnp.concatenate(lines, axis=0))
    lifted = product(high, place_ref[...]) + product(low, place_ref[...])
    for a in range(2):
        for g in range(groups):
            for q in range(PACK):
                plane = 2 * (g * PACK + q) + a
                line = (a * groups + g) * rows
                piece = lifted[line : line + rows, q * LANES : (q + 1) * LANES]
                out_ref[plane] = jnp.maximum(mid_ref[plane] + piece, 0.0)


def up_deep(me, blocks, weight, field, place, mid):
    return pl.pallas_call(
        functools.partial(up_deep_kernel, blocks),
        out_shape=jax.ShapeDtypeStruct(mid.shape, jnp.float32),
        in_specs=[SMEM] + [VMEM] * 4,
        out_specs=VMEM,
        scratch_shapes=[pltpu.VMEM(field.shape, jnp.bfloat16)] * 2,
        name="up_deep",
    )(me, weight, field, place, mid)


def up_mid_kernel(weight_ref, field_ref, place_ref, out_ref, field_high, field_low):
    step = pl.program_id(0)

    @pl.when(step == 0)
    def _():
        field = field_ref[...].reshape(-1, LANES).T
        field_high[...], field_low[...] = split_inside(field)

    lines = []
    for tap in range(4):
        weight_high, weight_low = split_inside(weight_ref[tap])
        lines.append(product_three(field_high[...], field_low[...], weight_high, weight_low))
    high, low = split_inside(jnp.concatenate(lines, axis=0).T)
    lifted = product(high, place_ref[...]) + product(low, place_ref[...])
    for a in range(2):

        @pl.when(step == a)
        def _():
            out_ref[:, a, :] = lifted


def up_mid(weights, field, place):
    chan_mid, chan_fine = weights.shape[1:]
    return pl.pallas_call(
        up_mid_kernel,
        out_shape=jax.ShapeDtypeStruct((chan_fine, 2, place.shape[1]), jnp.float32),
        grid=(2,),
        in_specs=[
            pl.BlockSpec((4, chan_mid, chan_fine), lambda a: (a, 0, 0)),
            pl.BlockSpec(field.shape, lambda a: (0, 0, 0)),
            pl.BlockSpec(place.shape, lambda a: (0, 0)),
        ],
        out_specs=pl.BlockSpec((chan_fine, 2, place.shape[1]), lambda a: (0, 0, 0)),
        scratch_shapes=[pltpu.VMEM((MID_CELLS, chan_mid), jnp.bfloat16)] * 2,
        name="up_mid",
    )(weights, field, place)


def swap(field, bit):
    count = lax.axis_size("wide")
    return lax.ppermute(field, "wide", [(i, i ^ bit) for i in range(count)])


def shards(fine_field, w_down_fine, w_conv_mid, w_down_mid, w_conv_deep, w_up_deep, w_up_mid):
    count = lax.axis_size("wide")
    me = lax.axis_index("wide")
    me_array = me.astype(jnp.int32).reshape(1)
    chips = count // 2
    bits = [1 << k for k in range(count.bit_length() - 1)]
    mid_local, chan_mid = w_conv_mid.shape[1:]
    deep_local, chan_deep = w_conv_deep.shape[1:]
    pick_fine = picker(1, YA, ZA)
    pick_mid = picker(PACK, MID_ROWS, MID_COLS)

    mid_input = down_fine(fine_field, pick_fine.T, w_down_fine)

    conv_high, conv_low = split_outside(w_conv_mid.reshape(27 * mid_local, chan_mid))
    down_weight = w_down_mid.reshape(8 * mid_local, chan_deep).T
    w_rows = w_up_deep.reshape(8 * deep_local, chan_mid).T.reshape(count, mid_local, 8 * deep_local)

    ring = list(range(0, chips, 2)) + list(range(chips - 1, 0, -2))
    ahead = [
        (2 * ring[k] + core, 2 * ring[(k + 1) % chips] + core) for core in range(2) for k in range(chips)
    ]
    behind = [(target, source) for source, target in ahead]

    half = chan_mid // 2
    steps = chips // 2
    front = back = mid_input
    running = None
    queue = [((mid_input,), 0, False), ((swap(mid_input, 1),), 0, True)]
    for step in range(1, steps):
        front = lax.ppermute(front, "wide", ahead)
        back = lax.ppermute(back, "wide", behind)
        if step > 1:
            given, queue = queue, []
            running = conv_mid(me_array, conv_high, conv_low, given, running, count)
            front, back, running = lax.optimization_barrier((front, back, running))
        queue += [((front,), -step, False), ((back,), step, False)]
        held = [((swap(front, 1),), -step, True), ((swap(back, 1),), step, True)]
        if step == 1:
            later = held
        else:
            queue = later + queue
            later = held
    upper = lax.ppermute(front[:half], "wide", ahead)
    lower = lax.ppermute(back[half:], "wide", behind)
    running = conv_mid(me_array, conv_high, conv_low, queue, running, count)
    given = later + [((upper, lower), steps, False), ((swap(upper, 1), swap(lower, 1)), steps, True)]
    mid_field, part = down_mid(me_array, conv_high, conv_low, pick_mid, down_weight, given, running, count)

    held = part
    for bit in bits[:-1]:
        size = held.shape[0] // 2
        mine = (me // bit) % 2
        keep = lax.dynamic_slice_in_dim(held, mine * size, size, 0)
        send = lax.dynamic_slice_in_dim(held, (1 - mine) * size, size, 0)
        held = keep + swap(send, bit)
    held = jax.nn.relu(held + swap(held, bits[-1]))
    for bit in bits[-2::-1]:
        held = jnp.concatenate([held, swap(held, bit)], axis=0)
    deep_output = conv_deep(me_array, count // 2, w_conv_deep.reshape(27 * deep_local, chan_deep), held)

    w_columns = lax.all_to_all(w_rows, "wide", split_axis=0, concat_axis=0, tiled=True)
    held = deep_output
    for bit in bits[::-1]:
        held = jnp.concatenate([held, swap(held, bit)], axis=0)
    merged = up_deep(me_array, count, w_columns, held, pick_mid.T, mid_field)

    plane = lax.all_to_all(merged, "wide", split_axis=0, concat_axis=0, tiled=True)
    return up_mid(w_up_mid, plane, pick_fine.T)


def solution(mesh):
    return jax.shard_map(
        shards,
        mesh=mesh,
        in_specs=(
            P(None, ("groups", "wide"), None),
            P(),
            P(None, "wide", None),
            P(None, "wide", None),
            P(None, "wide", None),
            P(None, "wide", None),
            P(),
        ),
        out_specs=P(None, ("groups", "wide"), None),
        check_vma=False,
    )
```

```python
import functools

import jax
import jax.numpy as jnp
import numpy as np
from jax import lax
from jax.experimental import pallas as pl
from jax.experimental.pallas import tpu as pltpu
from jax.sharding import PartitionSpec as P


YA = 32
ZA = 16
MID_ROWS, MID_COLS = YA // 2, ZA // 2
MID_CELLS = MID_ROWS * MID_COLS
DEEP_ROWS, DEEP_COLS = YA // 4, ZA // 4
DEEP_CELLS = DEEP_ROWS * DEEP_COLS
LANES = 128
PACK = LANES // DEEP_CELLS
SMEM = pl.BlockSpec(memory_space=pltpu.SMEM)
VMEM = pl.BlockSpec(memory_space=pltpu.VMEM)


def grant(mebibytes):
    return pltpu.CompilerParams(vmem_limit_bytes=int(mebibytes * 1024 * 1024))


def split_outside(weights):
    rounded = lax.reduce_precision(weights, 8, 7)
    return rounded.astype(jnp.bfloat16), (weights - rounded).astype(jnp.bfloat16)


def split_inside(values):
    high = values.astype(jnp.bfloat16)
    return high, (values - high.astype(jnp.float32)).astype(jnp.bfloat16)


def product(left, right):
    return jnp.dot(left, right, preferred_element_type=jnp.float32)


def product_three(left_high, left_low, right_high, right_low):
    return (
        product(left_high, right_high)
        + product(left_high, right_low)
        + product(left_low, right_high)
    )


def product_stacked(left_high, left_low, right_high, right_low):
    count = left_high.shape[0]
    both = product(jnp.concatenate([left_high, left_low], axis=0), right_high)
    return both[:count] + both[count:] + product(left_high, right_low)


def picker(blocks, rows, cols, xp=jnp):
    small_rows, small_cols = rows // 2, cols // 2
    big = xp.arange(blocks * rows * cols)[:, None]
    small = xp.arange(4 * blocks * small_rows * small_cols)[None, :]
    cells = small_rows * small_cols
    tap, block, cell = small // (blocks * cells), small // cells % blocks, small % cells
    row = 2 * (cell // small_cols) + tap // 2
    col = 2 * (cell % small_cols) + tap % 2
    return (big == (block * rows + row) * cols + col).astype(jnp.bfloat16)


def inside(places, limit, step):
    moved = places + step
    return (moved >= 0) & (moved < limit)


def down_fine_kernel(field_ref, place_ref, weight_ref, out_ref, total_ref):
    step = pl.program_id(0)
    for a in range(2):

        @pl.when(step == a)
        def _():
            high, low = [
                lax.dot_general(
                    place_ref[...], part, (((1,), (1,)), ((), ())), preferred_element_type=jnp.float32
                ).astype(jnp.bfloat16)
                for part in split_inside(field_ref[:, a, :])
            ]
            total = jnp.zeros(total_ref.shape, jnp.float32) if a == 0 else total_ref[...]
            for tap in range(4):
                weight_high, weight_low = split_inside(weight_ref[tap])
                block = slice(tap * MID_CELLS, (tap + 1) * MID_CELLS)
                total = total + product_stacked(high[block], low[block], weight_high, weight_low)
            if a == 0:
                total_ref[...] = total
            else:
                out_ref[...] = total.T


def down_fine(field, place, weights):
    chan_fine, chan_mid = weights.shape[1:]
    return pl.pallas_call(
        down_fine_kernel,
        out_shape=jax.ShapeDtypeStruct((chan_mid, MID_CELLS), jnp.float32),
        grid=(2,),
        in_specs=[
            pl.BlockSpec(field.shape, lambda a: (0, 0, 0)),
            pl.BlockSpec(place.shape, lambda a: (0, 0)),
            pl.BlockSpec((4, chan_fine, chan_mid), lambda a: (a, 0, 0)),
        ],
        out_specs=pl.BlockSpec((chan_mid, MID_CELLS), lambda a: (0, 0)),
        scratch_shapes=[pltpu.VMEM((MID_CELLS, chan_mid), jnp.float32)],
        name="down_fine",
        compiler_params=grant(60),
    )(field, place, weights)


def plane_at(me, step, other, chips):
    chip, core = me // 2, me % 2
    step = jnp.where(core == 0, -step, step)
    position = jnp.where(chip % 2 == 0, chip // 2, chips - 1 - chip // 2)
    position = (position + step + chips) % chips
    chip = jnp.where(position < chips // 2, 2 * position, 2 * (chips - 1 - position) + 1)
    return 2 * chip + (1 - core if other else core)


def conv_mid_add(me, chips, places, high_ref, low_ref, fields, sum_ref):
    rows = sum_ref.shape[1]
    field_high, field_low = split_inside(jnp.concatenate(fields, axis=1))
    place = lax.broadcasted_iota(jnp.int32, (rows, LANES), 1)
    row_of, col_of = place // MID_COLS, place % MID_COLS
    for a in range(3):
        block = pl.ds(a * 9 * rows, 9 * rows)
        spread = product_three(high_ref[block, :], low_ref[block, :], field_high, field_low)
        for side, (step, other) in enumerate(places):
            total = jnp.zeros((rows, LANES), jnp.float32)
            for b in range(3):
                for c in range(3):
                    tap = 3 * b + c
                    piece = spread[tap * rows : (tap + 1) * rows, side * LANES : (side + 1) * LANES]
                    offset = (b - 1) * MID_COLS + (c - 1)
                    if offset:
                        piece = pltpu.roll(piece, (-offset) % LANES, 1)
                        keep = inside(row_of, MID_ROWS, b - 1) & inside(col_of, MID_COLS, c - 1)
                        piece = jnp.where(keep, piece, 0.0)
                    total = total + piece
            plane = plane_at(me, step, other, chips) + (2 - a)
            sum_ref[plane] = sum_ref[plane] + total


def conv_mid_kernel(chips, places, first, me_ref, high_ref, low_ref, *refs):
    sum_ref, both_ref = refs[-2:]
    if first:
        sum_ref[...] = jnp.zeros_like(sum_ref)
    else:
        sum_ref[...] = refs[-3][...]
    fields, at = [], 0
    while len(fields) < len(places):
        field = refs[at][...]
        fields += [field] if field.shape[1] == LANES else [field[:, :LANES], field[:, LANES:]]
        at += 1
    both_ref[...] = jnp.concatenate(fields[-2:], axis=1)
    conv_mid_add(me_ref[0], chips, places, high_ref, low_ref, fields, sum_ref)


def conv_mid(me, high, low, fields, places, running, planes):
    rows = high.shape[0] // 27
    arrays = [me, high, low, *fields] + ([] if running is None else [running])
    return pl.pallas_call(
        functools.partial(conv_mid_kernel, planes // 2, places, running is None),
        out_shape=(
            jax.ShapeDtypeStruct((planes + 2, rows, LANES), jnp.float32),
            jax.ShapeDtypeStruct((high.shape[1], 2 * LANES), jnp.float32),
        ),
        in_specs=[SMEM] + [VMEM] * (len(arrays) - 1),
        out_specs=(VMEM, VMEM),
        input_output_aliases={} if running is None else {len(arrays) - 1: 0},
        name="conv_mid",
        compiler_params=grant(14),
    )(*arrays)


def down_mid_kernel(chips, places, me_ref, high_ref, low_ref, pick_ref, weight_ref, *refs):
    running_ref, mid_ref, keep_ref, send_ref, sum_ref, turned, weight_high, weight_low = refs[-8:]
    turned[...] = weight_ref[...].T
    sorted_split(me_ref[0], [turned], weight_high, weight_low, chips, False)
    sum_ref[...] = running_ref[...]
    fields = [refs[0][:, :LANES], refs[0][:, LANES:], refs[1][...], refs[2][...]]
    conv_mid_add(me_ref[0], chips, places, high_ref, low_ref, fields, sum_ref)
    planes = mid_ref.shape[0]
    groups = planes // 2 // PACK
    mid_ref[...] = jnp.maximum(sum_ref[1 : planes + 1], 0.0)
    rows = mid_ref.shape[1]
    lines = []
    for a in range(2):
        for g in range(groups):
            lines.append(jnp.concatenate([mid_ref[2 * (g * PACK + q) + a] for q in range(PACK)], axis=1))
    high, low = split_inside(jnp.concatenate(lines, axis=0))
    picks = []
    for part in (high, low):
        moved = product(part, pick_ref[...]).astype(jnp.bfloat16)
        taps = []
        for a in range(2):
            for tap in range(4):
                taps.append(
                    jnp.concatenate(
                        [
                            moved[(a * groups + g) * rows : (a * groups + g + 1) * rows, tap * LANES : (tap + 1) * LANES]
                            for g in range(groups)
                        ],
                        axis=1,
                    )
                )
        picks.append(jnp.concatenate(taps, axis=0))
    half = keep_ref.shape[0]
    part = product_three(weight_high[...], weight_low[...], picks[0], picks[1])
    keep_ref[...] = part[:half]
    send_ref[...] = part[half:]


def down_mid(me, high, low, pick, weight, fields, places, running, planes):
    rows = high.shape[0] // 27
    arrays = [me, high, low, pick, weight, *fields, running]
    half = jax.ShapeDtypeStruct((weight.shape[1] // 2, planes // 2 * DEEP_CELLS), jnp.float32)
    turned = (weight.shape[1], weight.shape[0])
    return pl.pallas_call(
        functools.partial(down_mid_kernel, planes // 2, places),
        out_shape=(jax.ShapeDtypeStruct((planes, rows, LANES), jnp.float32), half, half),
        in_specs=[SMEM] + [VMEM] * (len(arrays) - 1),
        out_specs=(VMEM, VMEM, VMEM),
        scratch_shapes=[pltpu.VMEM(running.shape, jnp.float32), pltpu.VMEM(turned, jnp.float32)]
        + [pltpu.VMEM(turned, jnp.bfloat16)] * 2,
        name="down_mid",
        compiler_params=grant(16),
    )(*arrays)


def reversed_bits(value, blocks):
    width = blocks.bit_length() - 1
    return sum(((value >> k) & 1) << (width - 1 - k) for k in range(width))


def sorted_split(me, pieces, high_ref, low_ref, blocks, whole):
    size = sum(piece.shape[0] for piece in pieces) // blocks
    at = 0
    for piece in pieces:
        for line in range(piece.shape[0] // size):
            high, low = split_inside(piece[pl.ds(line * size, size), :])
            target = reversed_bits(at, blocks) ^ me if whole else at ^ reversed_bits(me % blocks, blocks)
            target = pl.ds(pl.multiple_of(target * size, size), size)
            high_ref[target, :] = high
            low_ref[target, :] = low
            at += 1


def conv_deep_kernel(blocks, me_ref, high_ref, low_ref, near_ref, far_ref, out_ref, field_high, field_low):
    sorted_split(me_ref[0], [near_ref, far_ref], field_high, field_low, blocks, False)
    rows, cells = out_ref.shape
    place = lax.broadcasted_iota(jnp.int32, (rows, cells), 1)
    plane_of = place // DEEP_CELLS
    row_of, col_of = place // DEEP_COLS % DEEP_ROWS, place % DEEP_COLS
    summed = jnp.zeros((rows, cells), jnp.float32)
    for a in range(3):
        block = pl.ds(a * 9 * rows, 9 * rows)
        spread = product_three(high_ref[block, :], low_ref[block, :], field_high[...], field_low[...])
        total = jnp.zeros((rows, cells), jnp.float32)
        for b in range(3):
            for c in range(3):
                tap = 3 * b + c
                piece = spread[tap * rows : (tap + 1) * rows]
                offset = (b - 1) * DEEP_COLS + (c - 1)
                if offset:
                    piece = pltpu.roll(piece, (-offset) % cells, 1)
                    keep = inside(row_of, DEEP_ROWS, b - 1) & inside(col_of, DEEP_COLS, c - 1)
                    piece = jnp.where(keep, piece, 0.0)
                total = total + piece
        if a != 1:
            total = pltpu.roll(total, (-(a - 1) * DEEP_CELLS) % cells, 1)
            total = jnp.where(inside(plane_of, cells // DEEP_CELLS, a - 1), total, 0.0)
        summed = summed + total
    out_ref[...] = jnp.maximum(summed, 0.0)


def conv_deep(me, blocks, high, low, near, far):
    rows, cells = high.shape[0] // 27, near.shape[1]
    return pl.pallas_call(
        functools.partial(conv_deep_kernel, blocks),
        out_shape=jax.ShapeDtypeStruct((rows, cells), jnp.float32),
        in_specs=[SMEM] + [VMEM] * 4,
        out_specs=VMEM,
        scratch_shapes=[pltpu.VMEM((high.shape[1], cells), jnp.bfloat16)] * 2,
        name="conv_deep",
        compiler_params=grant(16),
    )(me, high, low, near, far)


def up_deep_kernel(blocks, me_ref, turn_ref, first_ref, second_ref, *refs):
    near_ref, far_ref, place_ref, mid_ref, out_ref, field_high, field_low = refs
    sorted_split(me_ref[0], [near_ref, far_ref], field_high, field_low, blocks, True)
    flip = turn_ref[0] != 0
    upper = jnp.where(flip, second_ref[...], first_ref[...])
    lower = jnp.where(flip, first_ref[...], second_ref[...])
    weight_rows = jnp.concatenate([upper, lower], axis=1)
    planes, rows, _ = mid_ref.shape
    groups = planes // 2 // PACK
    size = weight_rows.shape[2] // 8
    weight = jnp.concatenate(
        [
            jnp.concatenate([weight_rows[block, :, tap * size : (tap + 1) * size] for block in range(blocks)], axis=1)
            for tap in range(8)
        ],
        axis=0,
    )
    weight_high, weight_low = split_inside(weight)
    spread = product_three(weight_high, weight_low, field_high[...], field_low[...])
    lines = []
    for a in range(2):
        for g in range(groups):
            lines.append(
                jnp.concatenate(
                    [
                        spread[(4 * a + tap) * rows : (4 * a + tap + 1) * rows, g * LANES : (g + 1) * LANES]
                        for tap in range(4)
                    ],
                    axis=1,
                )
            )
    high, low = split_inside(jnp.concatenate(lines, axis=0))
    lifted = product(high, place_ref[...]) + product(low, place_ref[...])
    for a in range(2):
        for g in range(groups):
            for q in range(PACK):
                plane = 2 * (g * PACK + q) + a
                line = (a * groups + g) * rows
                piece = lifted[line : line + rows, q * LANES : (q + 1) * LANES]
                out_ref[plane] = jnp.maximum(mid_ref[plane] + piece, 0.0)


def up_deep(me, turn, blocks, first, second, near, far, place, mid):
    depth, cells = 2 * near.shape[0], near.shape[1]
    return pl.pallas_call(
        functools.partial(up_deep_kernel, blocks),
        out_shape=jax.ShapeDtypeStruct(mid.shape, jnp.float32),
        in_specs=[SMEM] * 2 + [VMEM] * 6,
        out_specs=VMEM,
        scratch_shapes=[pltpu.VMEM((depth, cells), jnp.bfloat16)] * 2,
        name="up_deep",
        compiler_params=grant(16),
    )(me, turn, first, second, near, far, place, mid)


def up_mid_kernel(high_ref, low_ref, field_ref, place_ref, out_ref):
    field_high, field_low = split_inside(field_ref[...].reshape(-1, LANES).T)
    for a in range(2):
        lines = [
            product_stacked(field_high, field_low, high_ref[4 * a + tap], low_ref[4 * a + tap]) for tap in range(4)
        ]
        high, low = split_inside(jnp.concatenate(lines, axis=0).T)
        out_ref[:, a, :] = product(high, place_ref[...]) + product(low, place_ref[...])


def up_mid(high, low, field, place):
    return pl.pallas_call(
        up_mid_kernel,
        out_shape=jax.ShapeDtypeStruct((high.shape[2], 2, place.shape[1]), jnp.float32),
        in_specs=[VMEM] * 4,
        out_specs=VMEM,
        name="up_mid",
        compiler_params=grant(16),
    )(high, low, field, place)


def turn_rows_kernel(turn_ref, weight_ref, out_ref):
    count, half, depth = out_ref.shape
    turned = weight_ref[...].T.reshape(count, 2, half, depth)
    out_ref[...] = jnp.where(turn_ref[0] != 0, turned[:, 1], turned[:, 0])


def turn_rows(turn, weight, count):
    depth, chan = weight.shape
    return pl.pallas_call(
        turn_rows_kernel,
        out_shape=jax.ShapeDtypeStruct((count, chan // count // 2, depth), jnp.float32),
        in_specs=[SMEM, VMEM],
        out_specs=VMEM,
        name="turn_rows",
        compiler_params=grant(8),
    )(turn, weight)


def join_kernel(near_ref, far_ref, out_ref):
    half = near_ref.shape[0]
    out_ref[:half] = near_ref[...]
    out_ref[half:] = far_ref[...]


def join(near, far):
    return pl.pallas_call(
        join_kernel,
        out_shape=jax.ShapeDtypeStruct((2 * near.shape[0], near.shape[1]), jnp.float32),
        in_specs=[VMEM] * 2,
        out_specs=VMEM,
        name="join",
        compiler_params=grant(4),
    )(near, far)


def swap(field, bit):
    count = lax.axis_size("wide")
    return lax.ppermute(field, "wide", [(i, i ^ bit) for i in range(count)])


def shards(fine_field, w_down_fine, w_conv_mid, w_down_mid, w_conv_deep, w_up_deep, w_up_mid):
    count = lax.axis_size("wide")
    me = lax.axis_index("wide")
    me_array = me.astype(jnp.int32).reshape(1)
    chips = count // 2
    bits = [1 << k for k in range(count.bit_length() - 1)]
    mid_local, chan_mid = w_conv_mid.shape[1:]
    deep_local, chan_deep = w_conv_deep.shape[1:]
    place_fine = jnp.asarray(picker(1, YA, ZA, np).T)
    pick_mid = picker(PACK, MID_ROWS, MID_COLS)

    mid_input = down_fine(fine_field, place_fine, w_down_fine)

    conv_high, conv_low = split_outside(w_conv_mid.reshape(27 * mid_local, chan_mid))
    down_weight = w_down_mid.reshape(8 * mid_local, chan_deep)
    turn_array = (lax.axis_index("groups") % 2).astype(jnp.int32).reshape(1)
    w_half = turn_rows(turn_array, w_up_deep.reshape(8 * deep_local, chan_mid), count)

    ring = list(range(0, chips, 2)) + list(range(chips - 1, 0, -2))
    links = [(2 * ring[k], 2 * ring[(k + 1) % chips]) for k in range(chips)]
    links += [(2 * ring[(k + 1) % chips] + 1, 2 * ring[k] + 1) for k in range(chips)]
    steps = chips // 2
    near, far = mid_input, swap(mid_input, 1)
    running = None
    fields, places = [near, far], [(0, False), (0, True)]
    for step in range(1, steps + 1):
        near = lax.ppermute(near, "wide", links)
        if step < steps:
            far = lax.ppermute(far, "wide", links)
        if step == 1:
            near, conv_high, conv_low = lax.optimization_barrier((near, conv_high, conv_low))
        else:
            running, both = conv_mid(me_array, conv_high, conv_low, fields, places, running, count)
            near, running = lax.optimization_barrier((near, running))
            fields, places = [swap(both, 1)], [(1 - step, True), (1 - step, False)]
        fields.append(near)
        places.append((step, False))
        if step < steps:
            fields.append(far)
            places.append((step, True))
    fields.append(swap(near, 1))
    places.append((-steps, True))
    mid_field, keep, send = down_mid(
        me_array, conv_high, conv_low, pick_mid, down_weight, fields, places, running, count
    )

    deep_high, deep_low = split_outside(w_conv_deep.reshape(27 * deep_local, chan_deep))
    held = keep + swap(send, 1)
    for bit in bits[1:-1]:
        size = held.shape[0] // 2
        held = held[:size] + swap(held[size:], bit)
        if bit == bits[1]:
            held, deep_high, deep_low = lax.optimization_barrier((held, deep_high, deep_low))
    held = jax.nn.relu(held + swap(held, bits[-1]))
    held, w_half = lax.optimization_barrier((held, w_half))
    for bit in bits[-2:0:-1]:
        held = join(held, swap(held, bit))
    w_near = lax.all_to_all(w_half, "wide", split_axis=0, concat_axis=0, tiled=True)
    deep_output = conv_deep(me_array, count // 2, deep_high, deep_low, held, swap(held, 1))

    deep_output, w_near = lax.optimization_barrier((deep_output, w_near))
    pairs = [(i, i ^ 1) for i in range(lax.axis_size("groups"))]
    w_far = lax.ppermute(w_near, "groups", pairs)
    last_high, last_low = split_outside(w_up_mid)
    held = deep_output
    for bit in bits[:0:-1]:
        held = join(held, swap(held, bit))
        if bit == bits[1]:
            held, last_high, last_low = lax.optimization_barrier((held, last_high, last_low))
    other = swap(held, 1)
    merged = up_deep(me_array, turn_array, count, w_near, w_far, held, other, pick_mid.T, mid_field)

    plane = lax.all_to_all(merged, "wide", split_axis=0, concat_axis=0, tiled=True)
    return up_mid(last_high, last_low, plane, place_fine)


def solution(mesh):
    return jax.shard_map(
        shards,
        mesh=mesh,
        in_specs=(
            P(None, ("groups", "wide"), None),
            P(),
            P(None, "wide", None),
            P(None, "wide", None),
            P(None, "wide", None),
            P(None, "wide", None),
            P(),
        ),
        out_specs=P(None, ("groups", "wide"), None),
        check_vma=False,
    )
```

```python
import functools

import jax
import jax.numpy as jnp
import numpy as np
from jax import lax
from jax.experimental import pallas as pl
from jax.experimental.pallas import tpu as pltpu
from jax.sharding import PartitionSpec as P


YA = 32
ZA = 16
MID_ROWS, MID_COLS = YA // 2, ZA // 2
MID_CELLS = MID_ROWS * MID_COLS
DEEP_ROWS, DEEP_COLS = YA // 4, ZA // 4
DEEP_CELLS = DEEP_ROWS * DEEP_COLS
LANES = 128
PACK = LANES // DEEP_CELLS
SMEM = pl.BlockSpec(memory_space=pltpu.SMEM)
VMEM = pl.BlockSpec(memory_space=pltpu.VMEM)


def grant(mebibytes):
    return pltpu.CompilerParams(vmem_limit_bytes=int(mebibytes * 1024 * 1024))


def split_outside(weights):
    rounded = lax.reduce_precision(weights, 8, 7)
    return rounded.astype(jnp.bfloat16), (weights - rounded).astype(jnp.bfloat16)


def split_inside(values):
    high = values.astype(jnp.bfloat16)
    return high, (values - high.astype(jnp.float32)).astype(jnp.bfloat16)


def product(left, right):
    return jnp.dot(left, right, preferred_element_type=jnp.float32)


def product_three(left_high, left_low, right_high, right_low):
    return (
        product(left_high, right_high)
        + product(left_high, right_low)
        + product(left_low, right_high)
    )


def product_stacked(left_high, left_low, right_high, right_low):
    count = left_high.shape[0]
    both = product(jnp.concatenate([left_high, left_low], axis=0), right_high)
    return both[:count] + both[count:] + product(left_high, right_low)


def picker(blocks, rows, cols, xp=jnp):
    small_rows, small_cols = rows // 2, cols // 2
    big = xp.arange(blocks * rows * cols)[:, None]
    small = xp.arange(4 * blocks * small_rows * small_cols)[None, :]
    cells = small_rows * small_cols
    tap, block, cell = small // (blocks * cells), small // cells % blocks, small % cells
    row = 2 * (cell // small_cols) + tap // 2
    col = 2 * (cell % small_cols) + tap % 2
    return (big == (block * rows + row) * cols + col).astype(jnp.bfloat16)


def inside(places, limit, step):
    moved = places + step
    return (moved >= 0) & (moved < limit)


def down_fine_kernel(field_ref, place_ref, weight_ref, out_ref, total_ref):
    step = pl.program_id(0)
    for a in range(2):

        @pl.when(step == a)
        def _():
            high, low = [
                lax.dot_general(
                    place_ref[...], part, (((1,), (1,)), ((), ())), preferred_element_type=jnp.float32
                ).astype(jnp.bfloat16)
                for part in split_inside(field_ref[:, a, :])
            ]
            total = jnp.zeros(total_ref.shape, jnp.float32) if a == 0 else total_ref[...]
            for tap in range(4):
                weight_high, weight_low = split_inside(weight_ref[tap])
                block = slice(tap * MID_CELLS, (tap + 1) * MID_CELLS)
                total = total + product_stacked(high[block], low[block], weight_high, weight_low)
            if a == 0:
                total_ref[...] = total
            else:
                out_ref[...] = total.T


def down_fine(field, place, weights):
    chan_fine, chan_mid = weights.shape[1:]
    return pl.pallas_call(
        down_fine_kernel,
        out_shape=jax.ShapeDtypeStruct((chan_mid, MID_CELLS), jnp.float32),
        grid=(2,),
        in_specs=[
            pl.BlockSpec(field.shape, lambda a: (0, 0, 0)),
            pl.BlockSpec(place.shape, lambda a: (0, 0)),
            pl.BlockSpec((4, chan_fine, chan_mid), lambda a: (a, 0, 0)),
        ],
        out_specs=pl.BlockSpec((chan_mid, MID_CELLS), lambda a: (0, 0)),
        scratch_shapes=[pltpu.VMEM((MID_CELLS, chan_mid), jnp.float32)],
        name="down_fine",
        compiler_params=grant(60),
    )(field, place, weights)


def plane_at(me, step, other, chips):
    chip, core = me // 2, me % 2
    step = jnp.where(core == 0, -step, step)
    position = jnp.where(chip % 2 == 0, chip // 2, chips - 1 - chip // 2)
    position = (position + step + chips) % chips
    chip = jnp.where(position < chips // 2, 2 * position, 2 * (chips - 1 - position) + 1)
    return 2 * chip + (1 - core if other else core)


def conv_mid_add(me, chips, places, high_ref, low_ref, fields, sum_ref):
    rows = sum_ref.shape[1]
    field_high, field_low = split_inside(jnp.concatenate(fields, axis=1))
    place = lax.broadcasted_iota(jnp.int32, (rows, LANES), 1)
    row_of, col_of = place // MID_COLS, place % MID_COLS
    for a in range(3):
        block = pl.ds(a * 9 * rows, 9 * rows)
        spread = product_three(high_ref[block, :], low_ref[block, :], field_high, field_low)
        for side, (step, other) in enumerate(places):
            total = jnp.zeros((rows, LANES), jnp.float32)
            for b in range(3):
                for c in range(3):
                    tap = 3 * b + c
                    piece = spread[tap * rows : (tap + 1) * rows, side * LANES : (side + 1) * LANES]
                    offset = (b - 1) * MID_COLS + (c - 1)
                    if offset:
                        piece = pltpu.roll(piece, (-offset) % LANES, 1)
                        keep = inside(row_of, MID_ROWS, b - 1) & inside(col_of, MID_COLS, c - 1)
                        piece = jnp.where(keep, piece, 0.0)
                    total = total + piece
            plane = plane_at(me, step, other, chips) + (2 - a)
            sum_ref[plane] = sum_ref[plane] + total


def conv_mid_kernel(chips, places, first, me_ref, high_ref, low_ref, *refs):
    sum_ref, both_ref = refs[-2:]
    if first:
        sum_ref[...] = jnp.zeros_like(sum_ref)
    else:
        sum_ref[...] = refs[-3][...]
    fields, at = [], 0
    while len(fields) < len(places):
        field = refs[at][...]
        fields += [field] if field.shape[1] == LANES else [field[:, :LANES], field[:, LANES:]]
        at += 1
    both_ref[...] = jnp.concatenate(fields[-2:], axis=1)
    conv_mid_add(me_ref[0], chips, places, high_ref, low_ref, fields, sum_ref)


def conv_mid(me, high, low, fields, places, running, planes):
    rows = high.shape[0] // 27
    arrays = [me, high, low, *fields] + ([] if running is None else [running])
    return pl.pallas_call(
        functools.partial(conv_mid_kernel, planes // 2, places, running is None),
        out_shape=(
            jax.ShapeDtypeStruct((planes + 2, rows, LANES), jnp.float32),
            jax.ShapeDtypeStruct((high.shape[1], 2 * LANES), jnp.float32),
        ),
        in_specs=[SMEM] + [VMEM] * (len(arrays) - 1),
        out_specs=(VMEM, VMEM),
        input_output_aliases={} if running is None else {len(arrays) - 1: 0},
        name="conv_mid",
        compiler_params=grant(14),
    )(*arrays)


def down_mid_kernel(chips, places, me_ref, high_ref, low_ref, pick_ref, weight_ref, *refs):
    running_ref, mid_ref, keep_ref, send_ref, sum_ref, turned, weight_high, weight_low = refs[-8:]
    turned[...] = weight_ref[...].T
    sorted_split(me_ref[0], [turned], weight_high, weight_low, chips, False)
    sum_ref[...] = running_ref[...]
    fields = [refs[0][:, :LANES], refs[0][:, LANES:], refs[1][...], refs[2][...]]
    conv_mid_add(me_ref[0], chips, places, high_ref, low_ref, fields, sum_ref)
    planes = mid_ref.shape[0]
    groups = planes // 2 // PACK
    mid_ref[...] = jnp.maximum(sum_ref[1 : planes + 1], 0.0)
    rows = mid_ref.shape[1]
    lines = []
    for a in range(2):
        for g in range(groups):
            lines.append(jnp.concatenate([mid_ref[2 * (g * PACK + q) + a] for q in range(PACK)], axis=1))
    high, low = split_inside(jnp.concatenate(lines, axis=0))
    picks = []
    for part in (high, low):
        moved = product(part, pick_ref[...]).astype(jnp.bfloat16)
        taps = []
        for a in range(2):
            for tap in range(4):
                taps.append(
                    jnp.concatenate(
                        [
                            moved[(a * groups + g) * rows : (a * groups + g + 1) * rows, tap * LANES : (tap + 1) * LANES]
                            for g in range(groups)
                        ],
                        axis=1,
                    )
                )
        picks.append(jnp.concatenate(taps, axis=0))
    half = keep_ref.shape[0]
    part = product_three(weight_high[...], weight_low[...], picks[0], picks[1])
    keep_ref[...] = part[:half]
    send_ref[...] = part[half:]


def down_mid(me, high, low, pick, weight, fields, places, running, planes):
    rows = high.shape[0] // 27
    arrays = [me, high, low, pick, weight, *fields, running]
    half = jax.ShapeDtypeStruct((weight.shape[1] // 2, planes // 2 * DEEP_CELLS), jnp.float32)
    turned = (weight.shape[1], weight.shape[0])
    return pl.pallas_call(
        functools.partial(down_mid_kernel, planes // 2, places),
        out_shape=(jax.ShapeDtypeStruct((planes, rows, LANES), jnp.float32), half, half),
        in_specs=[SMEM] + [VMEM] * (len(arrays) - 1),
        out_specs=(VMEM, VMEM, VMEM),
        scratch_shapes=[pltpu.VMEM(running.shape, jnp.float32), pltpu.VMEM(turned, jnp.float32)]
        + [pltpu.VMEM(turned, jnp.bfloat16)] * 2,
        name="down_mid",
        compiler_params=grant(16),
    )(*arrays)


def reversed_bits(value, blocks):
    width = blocks.bit_length() - 1
    return sum(((value >> k) & 1) << (width - 1 - k) for k in range(width))


def sorted_split(me, pieces, high_ref, low_ref, blocks, whole):
    size = sum(piece.shape[0] for piece in pieces) // blocks
    at = 0
    for piece in pieces:
        for line in range(piece.shape[0] // size):
            high, low = split_inside(piece[pl.ds(line * size, size), :])
            target = reversed_bits(at, blocks) ^ me if whole else at ^ reversed_bits(me % blocks, blocks)
            target = pl.ds(pl.multiple_of(target * size, size), size)
            high_ref[target, :] = high
            low_ref[target, :] = low
            at += 1


def conv_deep_kernel(blocks, me_ref, high_ref, low_ref, near_ref, far_ref, out_ref, field_high, field_low):
    sorted_split(me_ref[0], [near_ref, far_ref], field_high, field_low, blocks, False)
    rows, cells = out_ref.shape
    place = lax.broadcasted_iota(jnp.int32, (rows, cells), 1)
    plane_of = place // DEEP_CELLS
    row_of, col_of = place // DEEP_COLS % DEEP_ROWS, place % DEEP_COLS
    summed = jnp.zeros((rows, cells), jnp.float32)
    for a in range(3):
        block = pl.ds(a * 9 * rows, 9 * rows)
        spread = product_three(high_ref[block, :], low_ref[block, :], field_high[...], field_low[...])
        total = jnp.zeros((rows, cells), jnp.float32)
        for b in range(3):
            for c in range(3):
                tap = 3 * b + c
                piece = spread[tap * rows : (tap + 1) * rows]
                offset = (b - 1) * DEEP_COLS + (c - 1)
                if offset:
                    piece = pltpu.roll(piece, (-offset) % cells, 1)
                    keep = inside(row_of, DEEP_ROWS, b - 1) & inside(col_of, DEEP_COLS, c - 1)
                    piece = jnp.where(keep, piece, 0.0)
                total = total + piece
        if a != 1:
            total = pltpu.roll(total, (-(a - 1) * DEEP_CELLS) % cells, 1)
            total = jnp.where(inside(plane_of, cells // DEEP_CELLS, a - 1), total, 0.0)
        summed = summed + total
    out_ref[...] = jnp.maximum(summed, 0.0)


def conv_deep(me, blocks, high, low, near, far):
    rows, cells = high.shape[0] // 27, near.shape[1]
    return pl.pallas_call(
        functools.partial(conv_deep_kernel, blocks),
        out_shape=jax.ShapeDtypeStruct((rows, cells), jnp.float32),
        in_specs=[SMEM] + [VMEM] * 4,
        out_specs=VMEM,
        scratch_shapes=[pltpu.VMEM((high.shape[1], cells), jnp.bfloat16)] * 2,
        name="conv_deep",
        compiler_params=grant(16),
    )(me, high, low, near, far)


def up_deep_kernel(blocks, me_ref, turn_ref, first_ref, second_ref, *refs):
    near_ref, far_ref, place_ref, mid_ref, out_ref, field_high, field_low = refs
    sorted_split(me_ref[0], [near_ref, far_ref], field_high, field_low, blocks, True)
    flip = turn_ref[0] != 0
    upper = jnp.where(flip, second_ref[...], first_ref[...])
    lower = jnp.where(flip, first_ref[...], second_ref[...])
    weight_rows = jnp.concatenate([upper, lower], axis=1)
    planes, rows, _ = mid_ref.shape
    groups = planes // 2 // PACK
    size = weight_rows.shape[2] // 8
    weight = jnp.concatenate(
        [
            jnp.concatenate([weight_rows[block, :, tap * size : (tap + 1) * size] for block in range(blocks)], axis=1)
            for tap in range(8)
        ],
        axis=0,
    )
    weight_high, weight_low = split_inside(weight)
    spread = product_three(weight_high, weight_low, field_high[...], field_low[...])
    lines = []
    for a in range(2):
        for g in range(groups):
            lines.append(
                jnp.concatenate(
                    [
                        spread[(4 * a + tap) * rows : (4 * a + tap + 1) * rows, g * LANES : (g + 1) * LANES]
                        for tap in range(4)
                    ],
                    axis=1,
                )
            )
    high, low = split_inside(jnp.concatenate(lines, axis=0))
    lifted = product(high, place_ref[...]) + product(low, place_ref[...])
    for a in range(2):
        for g in range(groups):
            for q in range(PACK):
                plane = 2 * (g * PACK + q) + a
                line = (a * groups + g) * rows
                piece = lifted[line : line + rows, q * LANES : (q + 1) * LANES]
                out_ref[plane] = jnp.maximum(mid_ref[plane] + piece, 0.0)


def up_deep(me, turn, blocks, first, second, near, far, place, mid):
    depth, cells = 2 * near.shape[0], near.shape[1]
    return pl.pallas_call(
        functools.partial(up_deep_kernel, blocks),
        out_shape=jax.ShapeDtypeStruct(mid.shape, jnp.float32),
        in_specs=[SMEM] * 2 + [VMEM] * 6,
        out_specs=VMEM,
        scratch_shapes=[pltpu.VMEM((depth, cells), jnp.bfloat16)] * 2,
        name="up_deep",
        compiler_params=grant(16),
    )(me, turn, first, second, near, far, place, mid)


def up_mid_kernel(high_ref, low_ref, field_ref, place_ref, out_ref):
    field_high, field_low = split_inside(field_ref[...].reshape(-1, LANES).T)
    for a in range(2):
        lines = [
            product_stacked(field_high, field_low, high_ref[4 * a + tap], low_ref[4 * a + tap]) for tap in range(4)
        ]
        high, low = split_inside(jnp.concatenate(lines, axis=0).T)
        out_ref[:, a, :] = product(high, place_ref[...]) + product(low, place_ref[...])


def up_mid(high, low, field, place):
    return pl.pallas_call(
        up_mid_kernel,
        out_shape=jax.ShapeDtypeStruct((high.shape[2], 2, place.shape[1]), jnp.float32),
        in_specs=[VMEM] * 4,
        out_specs=VMEM,
        name="up_mid",
        compiler_params=grant(16),
    )(high, low, field, place)


def turn_rows_kernel(turn_ref, weight_ref, out_ref):
    count, half, depth = out_ref.shape
    turned = weight_ref[...].T.reshape(count, 2, half, depth)
    out_ref[...] = jnp.where(turn_ref[0] != 0, turned[:, 1], turned[:, 0])


def turn_rows(turn, weight, count):
    depth, chan = weight.shape
    return pl.pallas_call(
        turn_rows_kernel,
        out_shape=jax.ShapeDtypeStruct((count, chan // count // 2, depth), jnp.float32),
        in_specs=[SMEM, VMEM],
        out_specs=VMEM,
        name="turn_rows",
        compiler_params=grant(60),
    )(turn, weight)


def join_kernel(*refs):
    size = refs[0].shape[0]
    for at, piece in enumerate(refs[:-1]):
        refs[-1][at * size : (at + 1) * size] = piece[...]


def join(pieces):
    size, cells = pieces[0].shape
    return pl.pallas_call(
        join_kernel,
        out_shape=jax.ShapeDtypeStruct((len(pieces) * size, cells), jnp.float32),
        in_specs=[VMEM] * len(pieces),
        out_specs=VMEM,
        name="join",
        compiler_params=grant(4),
    )(*pieces)


def scatter(held, bits):
    parts = jnp.split(held, 1 << len(bits), axis=0)
    offsets = [0]
    for bit in bits[::-1]:
        offsets += [offset ^ bit for offset in offsets]
    total = parts[0]
    for part, offset in list(zip(parts, offsets))[1:]:
        total = total + swap(part, offset)
    return total


def gather(held, bits):
    offsets = [0]
    for bit in bits[::-1]:
        offsets += [offset ^ bit for offset in offsets]
    return join([held] + [swap(held, offset) for offset in offsets[1:]])


def swap(field, bit):
    count = lax.axis_size("wide")
    return lax.ppermute(field, "wide", [(i, i ^ bit) for i in range(count)])


def shards(fine_field, w_down_fine, w_conv_mid, w_down_mid, w_conv_deep, w_up_deep, w_up_mid):
    count = lax.axis_size("wide")
    me = lax.axis_index("wide")
    me_array = me.astype(jnp.int32).reshape(1)
    chips = count // 2
    bits = [1 << k for k in range(count.bit_length() - 1)]
    mid_local, chan_mid = w_conv_mid.shape[1:]
    deep_local, chan_deep = w_conv_deep.shape[1:]
    place_fine = jnp.asarray(picker(1, YA, ZA, np).T)
    pick_mid = picker(PACK, MID_ROWS, MID_COLS)

    turn_array = (lax.axis_index("groups") % 2).astype(jnp.int32).reshape(1)
    w_half = turn_rows(turn_array, w_up_deep.reshape(8 * deep_local, chan_mid), count)
    w_near = lax.all_to_all(w_half, "wide", split_axis=0, concat_axis=0, tiled=True)
    mid_input = down_fine(fine_field, place_fine, w_down_fine)

    conv_high, conv_low = split_outside(w_conv_mid.reshape(27 * mid_local, chan_mid))
    down_weight = w_down_mid.reshape(8 * mid_local, chan_deep)

    ring = list(range(0, chips, 2)) + list(range(chips - 1, 0, -2))
    links = [(2 * ring[k], 2 * ring[(k + 1) % chips]) for k in range(chips)]
    links += [(2 * ring[(k + 1) % chips] + 1, 2 * ring[k] + 1) for k in range(chips)]
    steps = chips // 2
    near, far = mid_input, swap(mid_input, 1)
    running = None
    fields, places = [near, far], [(0, False), (0, True)]
    for step in range(1, steps + 1):
        near = lax.ppermute(near, "wide", links)
        if step < steps:
            far = lax.ppermute(far, "wide", links)
        if step == 1:
            near, conv_high, conv_low = lax.optimization_barrier((near, conv_high, conv_low))
        else:
            running, both = conv_mid(me_array, conv_high, conv_low, fields, places, running, count)
            near, running = lax.optimization_barrier((near, running))
            fields, places = [swap(both, 1)], [(1 - step, True), (1 - step, False)]
        fields.append(near)
        places.append((step, False))
        if step < steps:
            fields.append(far)
            places.append((step, True))
    fields.append(swap(near, 1))
    places.append((-steps, True))
    mid_field, keep, send = down_mid(
        me_array, conv_high, conv_low, pick_mid, down_weight, fields, places, running, count
    )

    deep_high, deep_low = split_outside(w_conv_deep.reshape(27 * deep_local, chan_deep))
    held = keep + swap(send, 1)
    groups = [bits[at : min(at + 2, len(bits) - 1)] for at in range(1, len(bits) - 1, 2)]
    for group in groups:
        held = scatter(held, group)
    held, w_near = lax.optimization_barrier((held, w_near))
    pairs = [(i, i ^ 1) for i in range(lax.axis_size("groups"))]
    w_far = lax.ppermute(w_near, "groups", pairs)
    held = jax.nn.relu(held + swap(held, bits[-1]))
    held, deep_high, deep_low = lax.optimization_barrier((held, deep_high, deep_low))
    for group in groups[::-1]:
        held = gather(held, group)
    deep_output = conv_deep(me_array, count // 2, deep_high, deep_low, held, swap(held, 1))

    last_high, last_low = split_outside(w_up_mid)
    held = gather(deep_output, bits[-1:])
    for group in groups[::-1]:
        held = gather(held, group)
    held, last_high, last_low = lax.optimization_barrier((held, last_high, last_low))
    other = swap(held, 1)
    merged = up_deep(me_array, turn_array, count, w_near, w_far, held, other, pick_mid.T, mid_field)

    plane = lax.all_to_all(merged, "wide", split_axis=0, concat_axis=0, tiled=True)
    return up_mid(last_high, last_low, plane, place_fine)


def solution(mesh):
    return jax.shard_map(
        shards,
        mesh=mesh,
        in_specs=(
            P(None, ("groups", "wide"), None),
            P(),
            P(None, "wide", None),
            P(None, "wide", None),
            P(None, "wide", None),
            P(None, "wide", None),
            P(),
        ),
        out_specs=P(None, ("groups", "wide"), None),
        check_vma=False,
    )
```
